32 devices in a mesh: map: 8 (over z, x), lay: 4 (over y, core).
Axes of the slice: x: 2, y: 2, z: 4, core: 2. Of those that a mesh axis runs over, the one named last changes fastest.
Arguments:
- temp_start: float32 [64, 64, 1024], P('lay', 'map'), may hold values from -6 to 6
- heating: bfloat16 [64, 64, 1024], P('lay', 'map'), may hold values from 0.099609375 to 2
- phase: int32 [64, 64, 1024], P('lay', 'map'), may hold values 0 or 1
- velocity: float32 [2, 64, 1024], P(None, 'map'), may hold values from -0.4 to 0.4
- surface: float32 [64, 1024], P('map'), may hold values from -6 to 6
- flux_start: float32 [64, 1024], P('map', 'lay'), may hold values from 0.5 to 1.5
- flux_prior: float32 [64, 1024], P('map', 'lay'), may hold values from 0 to 2
- basal_obs: float32 [64, 1024], P('map', 'lay'), may hold values from -6 to 6
- obs_mask: int32 [64, 1024], P('map', 'lay'), may hold values 0 or 1
Outputs:
- flux: float32 [64, 1024], P('map', 'lay')
- basal: float32 [64, 1024], P('map', 'lay')
The draws below stay inside these ranges and needn't reach their ends.
All inputs are finite; a program needn't handle non-finite values. No bound on the sum of `phase` or of `obs_mask` on one device may be relied on, other than what follows from the above.
Results may differ from the reference program's by a relative error of at most 0.0003.
Values sent between devices are 32-bit elements; how exact they have to be, the bound alone decides.
A program may use at most 64 MiB of HBM per device.

```python
import math
import jax
import jax.numpy as jnp

NX = 1024
NZ = 64
NSTEP = 2
ITERS = 2
NY = 64


def plant(drawn, stream_key, smallest, largest):
    longest = drawn.shape.index(max(drawn.shape))
    spots = []
    for shift in (0, 1):
        where = [jax.random.randint(jax.random.fold_in(stream_key, axis), (), 0, length) for axis, length in enumerate(drawn.shape)]
        where[longest] = (where[longest] + shift) % drawn.shape[longest]
        spots.append(tuple(where))
    return drawn.at[spots[0]].set(smallest).at[spots[1]].set(largest)


def levels(rng, dims, shards, smallest, largest):
    factor_of, own = 1.0, jax.random.fold_in(rng, 6)
    for axis_at, parts in shards:
        steps = jnp.exp(jax.random.uniform(jax.random.fold_in(own, axis_at), (parts,), jnp.float32, smallest / len(shards), largest / len(shards)))
        factor_of = factor_of * jnp.repeat(steps, dims[axis_at] // parts).reshape([-1 if axis == axis_at else 1 for axis in range(len(dims))])
    return factor_of


def bell_draw(key, extent, deviation, limit, shards=(), kind=jnp.bfloat16):
    loudness = levels(key, extent, shards, -0.22, 0.18) if shards else 1.0
    drawn = jax.random.normal(key, extent, jnp.float32) * deviation * loudness
    return jnp.minimum(jnp.maximum(drawn, -limit), limit).astype(kind)


def setup_inputs(seed: int = 0) -> dict:
    splits = jax.random.split(jax.random.key(seed), 10)
    temp_start = bell_draw(splits[0], (NZ, NY, NX), 1.0, 6.0, ((0, 4), (1, 8)), jnp.float32)
    heating = jnp.clip(jnp.exp(math.log(2.0) - 2.9996462 * jax.random.uniform(splits[1], (NZ, NY, NX), jnp.float32) ** levels(splits[1], (NZ, NY, NX), ((0, 4), (1, 8)), -0.2, 0.2)), 0.099609375, 2.0).astype(jnp.bfloat16)
    phase = plant((jax.random.randint(splits[2], (NZ, NY, NX), 0, 3) < 1).astype(jnp.int32), jax.random.fold_in(splits[2], 1), 0, 1)
    velocity = jnp.clip(jax.random.uniform(splits[3], (2, NY, NX), jnp.float32, -0.4, 0.4) * levels(splits[3], (2, NY, NX), ((1, 8),), -0.4, 0.0), -0.4, 0.4)
    surface = bell_draw(splits[4], (NY, NX), 1.0, 6.0, ((0, 8),), jnp.float32)
    flux_start = jnp.clip(0.5 + 1.0 * jax.random.uniform(splits[5], (NY, NX), jnp.float32) ** levels(splits[5], (NY, NX), ((0, 8), (1, 4)), -0.2, 0.2), 0.5, 1.5)
    flux_prior = jnp.clip(2.0 * jax.random.uniform(splits[6], (NY, NX), jnp.float32) ** levels(splits[6], (NY, NX), ((0, 8), (1, 4)), -0.2, 0.2), 0.0, 2.0)
    basal_obs = bell_draw(splits[7], (NY, NX), 1.0, 6.0, ((0, 8), (1, 4)), jnp.float32)
    obs_mask = plant((jax.random.randint(splits[8], (NY, NX), 0, 2) < 1).astype(jnp.int32), jax.random.fold_in(splits[8], 1), 0, 1)
    return {"temp_start": temp_start, "heating": heating, "phase": phase, "velocity": velocity, "surface": surface, "flux_start": flux_start, "flux_prior": flux_prior, "basal_obs": basal_obs, "obs_mask": obs_mask}


def kappa_of(phase):
    return jnp.where(phase == 1, 0.3, 1.0).astype(jnp.float32)


def factors(phase, rcoef):
    kap = kappa_of(phase)
    kup = jnp.concatenate([0.5 * (kap[:-1] + kap[1:]), kap[-1:]], axis=0)
    kdn = jnp.concatenate([jnp.zeros_like(kap[:1]), kup[:-1]], axis=0)
    diag = 1.0 + rcoef * (kdn + kup)
    off = -rcoef * kup
    depth = phase.shape[0]
    cps = []
    invs = []
    inv = 1.0 / diag[0]
    cps.append(off[0] * inv)
    invs.append(inv)
    for k in range(1, depth):
        den = diag[k] - off[k - 1] * cps[k - 1]
        inv = 1.0 / den
        invs.append(inv)
        cps.append(off[k] * inv)
    return cps, invs, off


def solve(rhs, fac):
    cps, invs, off = fac
    depth = len(cps)
    dps = [rhs[0] * invs[0]]
    for k in range(1, depth):
        dps.append((rhs[k] - off[k - 1] * dps[k - 1]) * invs[k])
    out = [None] * depth
    out[depth - 1] = dps[depth - 1]
    for k in range(depth - 2, -1, -1):
        out[k] = dps[k] - cps[k] * out[k + 1]
    return jnp.stack(out, axis=0)


def coeffs(velocity, shape):
    u = velocity[0]
    v = velocity[1]
    px = jnp.maximum(u, 0.0) * shape
    mx = jnp.maximum(-u, 0.0) * shape
    py = jnp.maximum(v, 0.0) * shape
    my = jnp.maximum(-v, 0.0) * shape
    return px, mx, py, my


def advect(f, co):
    px, mx, py, my = co
    diag = 1.0 - px - mx - py - my
    fp = jnp.pad(f, ((0, 0), (1, 1), (1, 1)))
    left = fp[:, 1:-1, :-2]
    right = fp[:, 1:-1, 2:]
    down = fp[:, :-2, 1:-1]
    upper = fp[:, 2:, 1:-1]
    return diag * f + px * left + mx * right + py * down + my * upper


def advect_back(w, co):
    px, mx, py, my = co
    diag = 1.0 - px - mx - py - my
    a_pad = jnp.pad(px * w, ((0, 0), (0, 0), (1, 1)))
    b_pad = jnp.pad(mx * w, ((0, 0), (0, 0), (1, 1)))
    c_pad = jnp.pad(py * w, ((0, 0), (1, 1), (0, 0)))
    d_pad = jnp.pad(my * w, ((0, 0), (1, 1), (0, 0)))
    return diag * w + a_pad[:, :, 2:] + b_pad[:, :, :-2] + c_pad[:, 2:, :] + d_pad[:, :-2, :]


def with_base(rhs, src):
    return jnp.concatenate([rhs[:1] + src[None], rhs[1:]], axis=0)


def reference(temp_start, heating, phase, velocity, surface, flux_start, flux_prior, basal_obs, obs_mask):
    depth = temp_start.shape[0]
    rcoef = depth * depth / 4.0
    dtime = rcoef / (depth * depth)
    beta = rcoef / depth
    rho = 0.5
    shape = (0.3 + 0.7 * (jnp.arange(depth).astype(jnp.float32) + 0.5) / depth)[:, None, None]
    co = coeffs(velocity, shape)
    fac = factors(phase, rcoef)
    kap_top = kappa_of(phase[-1])
    forced = dtime * heating.astype(jnp.float32)
    forced = jnp.concatenate([forced[:-1], (forced[-1] + rcoef * kap_top * surface)[None]], axis=0)
    flux = flux_start
    src = beta * flux
    temp = temp_start
    for step in range(NSTEP):
        temp = solve(with_base(advect(temp, co) + forced, src), fac)
    basal = temp[0]
    maskf = obs_mask.astype(jnp.float32)
    zeros = jnp.zeros_like(temp_start)
    for it in range(ITERS):
        misfit = maskf * (basal - basal_obs)
        lam = solve(with_base(zeros, misfit), fac)
        gsum = lam[0]
        for step in range(NSTEP - 1):
            lam = solve(advect_back(lam, co), fac)
            gsum = gsum + lam[0]
        grad = beta * gsum + rho * (flux - flux_prior)
        gnorm = jnp.sum(grad * grad)
        direc = -grad
        dsrc = beta * direc
        resp = solve(with_base(zeros, dsrc), fac)
        for step in range(NSTEP - 1):
            resp = solve(with_base(advect(resp, co), dsrc), fac)
        dbase = resp[0]
        curv = jnp.sum(maskf * dbase * dbase)
        alpha = gnorm / (curv + rho * gnorm)
        flux = flux + alpha * direc
        basal = basal + alpha * dbase
    return flux, basal
```

```python
import functools

import jax
import jax.numpy as jnp
from jax import lax
from jax.experimental import pallas as pl
from jax.experimental.pallas import tpu as pltpu
from jax.sharding import PartitionSpec as P

MESH = pl.DeviceIdType.MESH
F32 = jnp.float32
MARGIN = 128
HALO = 4
RHO = 0.5
(PHASE, HEAT, RHS, T_DN, T_UP, G_DN, G_UP, MEET1, MEET2, SUM1, SUM2,
 E_DN, E_UP, H1_DN, H1_UP, H2_DN, H2_UP, TILE, MAPS) = range(19)
NSEM = MAPS + 12


def lane(x, shift):
    n = x.shape[-1]
    col = lax.broadcasted_iota(jnp.int32, x.shape, x.ndim - 1)
    edge = 0 if shift > 0 else n - 1
    return jnp.where(col == edge, 0.0, pltpu.roll(x, shift % n, x.ndim - 1))


def row(x, shift, fill):
    n = x.shape[0]
    r = lax.broadcasted_iota(jnp.int32, x.shape, 0)
    edge = 0 if shift > 0 else n - 1
    return jnp.where(r == edge, fill, pltpu.roll(x, shift % n, 0))


def kernel(
    nmap, nlay,
    temp, heating, phase, velocity, surface, flux_in, prior_in, obs_in, mask_in,
    flux_out, basal_out,
    pb, hf, hb, rf, rb, tdn, tup, inv, cc, yy, gg, sgl, sgr, sgu, sgd, wg, gdn, gup,
    m1s, m1r, m2s, m2r, q1s, q1r, q2s, q2r, h1dn, h1up, h2dn, h2up,
    maps, maski, es, edn, eup, fields, tile, sc_s, sc_r,
    ssem, rsem, lsem, sc_ssem, sc_rsem,
):
    nzd, rows, width = temp.shape
    win = pb.shape[2]
    depth = nzd * nlay
    half = 2 * nzd
    part = flux_in.shape[1]
    rcoef = depth * depth / 4.0
    dtime = rcoef / (depth * depth)
    beta = rcoef / depth
    m = lax.axis_index("map")
    lay = lax.axis_index("lay")
    y = lay // 2
    c = lay % 2
    core_lay = y * 2 + (1 - c)
    far_lay = (1 - y) * 2 + c
    step_win = width - win
    mine = pl.multiple_of(c * step_win, 128)
    theirs = pl.multiple_of((1 - c) * step_win, 128)
    has_dn = m > 0
    has_up = m < nmap - 1

    def slot(j):
        return jnp.where(y == 0, j, half - 1 - j)

    def rcopy(src, dst, k, mm, ll):
        return pltpu.make_async_remote_copy(
            src_ref=src, dst_ref=dst, send_sem=ssem.at[k], recv_sem=rsem.at[k],
            device_id={"map": mm, "lay": ll}, device_id_type=MESH)

    ngroup = 2 * nmap
    me_g = m * 2 + c

    def peer(d):
        g = lax.rem(me_g + d, ngroup)
        return g // 2, y * 2 + lax.rem(g, 2)

    barrier = pltpu.get_barrier_semaphore()

    def greet(d, carry):
        mm, ll = peer(d)
        pl.semaphore_signal(barrier, inc=1, device_id={"map": mm, "lay": ll}, device_id_type=MESH)
        return carry

    lax.fori_loop(1, ngroup, greet, 0)
    for ll in (far_lay, (1 - y) * 2 + (1 - c)):
        pl.semaphore_signal(barrier, inc=1, device_id={"map": m, "lay": ll}, device_id_type=MESH)
    pl.semaphore_wait(barrier, ngroup - 1 + 2)

    both = []
    ph = rcopy(phase.at[:, :, pl.ds(theirs, win)], pb.at[pl.ds(c * nzd, nzd)], PHASE, m, core_lay)
    ph.start()
    ph_own = pltpu.make_async_copy(
        phase.at[:, :, pl.ds(mine, win)], pb.at[pl.ds(c * nzd, nzd)], lsem.at[0])
    ph_own.start()

    def to_up(src, dst, k):
        @pl.when(has_up)
        def _():
            rcopy(src, dst, k, m + 1, lay).start()

    def to_dn(src, dst, k):
        @pl.when(has_dn)
        def _():
            rcopy(src, dst, k, m - 1, lay).start()

    def done_up(src, dst, k):
        @pl.when(has_up)
        def _():
            rcopy(src, dst, k, m + 1, lay).wait_send()

        @pl.when(has_dn)
        def _():
            rcopy(src, dst, k, m - 1, lay).wait_recv()

    def done_dn(src, dst, k):
        @pl.when(has_dn)
        def _():
            rcopy(src, dst, k, m - 1, lay).wait_send()

        @pl.when(has_up)
        def _():
            rcopy(src, dst, k, m + 1, lay).wait_recv()

    t_up = (temp.at[:, rows - 1:rows, :], tdn, T_UP)
    t_dn = (temp.at[:, 0:1, :], tup, T_DN)
    to_up(*t_up)
    to_dn(*t_dn)

    map_srcs = (flux_in, prior_in, obs_in, mask_in)
    here = pl.multiple_of(lay * part, 128)
    map_copies = []
    for i, src in enumerate(map_srcs):
        dst = maski.at[:, pl.ds(here, part)] if i == 3 else maps.at[i, :, pl.ds(here, part)]
        own = pltpu.make_async_copy(src, dst, lsem.at[1 + i])
        own.start()
        map_copies.append(own)
        for d in range(1, nlay):
            cp = rcopy(src, dst, MAPS + 3 * i + d - 1, m, lax.rem(lay + d, nlay))
            cp.start()
            map_copies.append(cp)

    @pl.when(jnp.logical_not(has_dn))
    def _():
        for ref in (tdn, gdn, edn, h1dn, h2dn):
            ref[...] = jnp.zeros(ref.shape, F32)

    @pl.when(jnp.logical_not(has_up))
    def _():
        for ref in (tup, gup, eup, h1up, h2up):
            ref[...] = jnp.zeros(ref.shape, F32)

    def kappa(p):
        return jnp.where(p == 1, 0.3, 1.0).astype(F32)

    def heat(l, carry):
        hf[l] = dtime * heating[l].astype(F32)
        return carry

    lax.fori_loop(0, nzd, heat, 0)
    is_top = lay == nlay - 1
    hf[nzd - 1] += jnp.where(is_top, rcoef, 0.0) * kappa(phase[nzd - 1]) * surface[...]
    ht = rcopy(hf.at[:, :, pl.ds(theirs, win)], hb.at[pl.ds(c * nzd, nzd)], HEAT, m, core_lay)
    ht.start()
    ht_own = pltpu.make_async_copy(
        hf.at[:, :, pl.ds(mine, win)], hb.at[pl.ds(c * nzd, nzd)], lsem.at[5])
    ht_own.start()

    ph_own.wait()
    ph.wait()
    kap0 = kappa(pb[slot(0)])
    q0 = jnp.where(y == 1, rcoef, 0.0) * kap0
    g0 = jnp.where(y == 0, 1.0, 0.0) * jnp.ones_like(kap0)

    def eliminate(j, carry):
        kap, q, yg = carry
        kap_next = kappa(pb[slot(j + 1)])
        n = (0.5 * rcoef) * (kap + kap_next)
        iv = 1.0 / (1.0 + q + n)
        cj = n * iv
        inv[j] = iv
        cc[j] = cj
        yy[j] = yg
        return kap_next, cj * (1.0 + q), cj * yg

    kap_m, q_m, yg_m = lax.fori_loop(0, half - 1, eliminate, (kap0, q0, g0))
    m1s[0] = kap_m
    m1s[1] = 1.0 + q_m
    m1s[2] = yg_m
    meet1 = rcopy(m1s, m1r, MEET1, m, far_lay)
    meet1.start()

    done_up(*t_up)
    done_dn(*t_dn)

    def advect(l, carry):
        t = temp[l]
        z = (lay * nzd + l).astype(F32)
        sh = 0.3 + 0.7 * (z + 0.5) / depth
        u = velocity[0]
        v = velocity[1]
        flow = (
            jnp.maximum(u, 0.0) * lane(t, 1)
            + jnp.maximum(-u, 0.0) * lane(t, -1)
            + jnp.maximum(v, 0.0) * row(t, 1, tdn[l])
            + jnp.maximum(-v, 0.0) * row(t, -1, tup[l])
            - (jnp.abs(u) + jnp.abs(v)) * t
        )
        rf[l] = t + sh * flow + hf[l]
        return carry

    lax.fori_loop(0, nzd, advect, 0)
    rh = rcopy(rf.at[:, :, pl.ds(theirs, win)], rb.at[pl.ds(c * nzd, nzd)], RHS, m, core_lay)
    rh.start()
    rh_own = pltpu.make_async_copy(
        rf.at[:, :, pl.ds(mine, win)], rb.at[pl.ds(c * nzd, nzd)], lsem.at[6])
    rh_own.start()

    meet1.wait()
    n_mid = (0.5 * rcoef) * (kap_m + m1r[0])
    d_own = m1s[1] + n_mid
    d_far = m1r[1] + n_mid
    idet = 1.0 / (d_own * d_far - n_mid * n_mid)
    w_own = d_far * idet
    w_far = n_mid * idet
    gm = w_own * m1s[2] + w_far * m1r[2]
    gg[slot(half - 1)] = gm

    def back_g(i, x):
        j = half - 2 - i
        x = yy[j] * inv[j] + cc[j] * x
        gg[slot(j)] = x
        return x

    lax.fori_loop(0, half - 1, back_g, gm)
    g_up = (gg.at[:, rows - 1:rows, :], gdn, G_UP)
    g_dn = (gg.at[:, 0:1, :], gup, G_DN)
    to_up(*g_up)
    to_dn(*g_dn)

    for cp in map_copies:
        cp.wait()
    fx = maps[0, :, pl.ds(mine, win)]
    ob = maps[2, :, pl.ds(mine, win)]
    uw = velocity[0, :, pl.ds(mine, win)]
    vw = velocity[1, :, pl.ds(mine, win)]
    es[0] = fx - maps[1, :, pl.ds(mine, win)]
    es[1] = ob
    es[2] = maski[:, pl.ds(mine, win)].astype(F32)
    es[3] = uw
    es[4] = vw
    last = slice(rows - HALO, rows)
    first = slice(0, HALO)
    e_up = (es.at[:, last, :], edn, E_UP)
    e_dn = (es.at[:, first, :], eup, E_DN)
    to_up(*e_up)
    to_dn(*e_dn)

    rh_own.wait()
    rh.wait()
    y0 = rb[slot(0)] + jnp.where(y == 0, beta, 0.0) * fx

    def forward(j, x):
        yy[j] = x
        return rb[slot(j + 1)] + cc[j] * x

    y_m = lax.fori_loop(0, half - 1, forward, y0)
    m2s[...] = y_m
    meet2 = rcopy(m2s, m2r, MEET2, m, far_lay)
    meet2.start()

    ht_own.wait()
    ht.wait()
    done_up(*g_up)
    done_dn(*g_dn)
    suv = jnp.abs(uw) + jnp.abs(vw)

    def profile(k, carry):
        ad, ax, ay, af = carry
        g = gg[k]
        sh = 0.3 + 0.7 * ((y * half + k).astype(F32) + 0.5) / depth
        sg = sh * g
        left = lane(sg, 1)
        below = row(sg, 1, sh * gdn[k])
        w = g - suv * sg
        sgl[k] = left
        sgr[k] = lane(sg, -1)
        sgd[k] = below
        sgu[k] = row(sg, -1, sh * gup[k])
        wg[k] = w
        return ad + w * g, ax + left * g, ay + below * g, af + g * hb[k]

    zero = jnp.zeros((rows, win), F32)
    ad, ax, ay, af = lax.fori_loop(0, half, profile, (zero, zero, zero, zero))
    base = jnp.where(y == 0, 1.0, 0.0) * gg[0]
    q1s[0] = ad + base
    q1s[1] = ax
    q1s[2] = ay
    sum1 = rcopy(q1s, q1r, SUM1, m, far_lay)
    sum1.start()

    meet2.wait()
    x_m = w_own * y_m + w_far * m2r[...]

    def products(x, k, acc):
        a0, xr, xl, yu, yd = acc
        return (a0 + wg[k] * x, xr + sgr[k] * x, xl + sgl[k] * x,
                yu + sgu[k] * x, yd + sgd[k] * x)

    def back_t(i, carry):
        x, acc = carry
        j = half - 2 - i
        x = yy[j] * inv[j] + cc[j] * x
        return x, products(x, slot(j), acc)

    acc = products(x_m, slot(half - 1), (af, zero, zero, zero, zero))
    _, (a0, xr, xl, yu, yd) = lax.fori_loop(0, half - 1, back_t, (x_m, acc))
    none = jnp.zeros((1, win), F32)
    q2s[0] = (
        a0 + beta * fx * base
        + jnp.maximum(uw, 0.0) * lane(xr, 1) + jnp.maximum(-uw, 0.0) * lane(xl, -1)
        + jnp.maximum(vw, 0.0) * row(yu, 1, none) + jnp.maximum(-vw, 0.0) * row(yd, -1, none)
    )
    r = lax.broadcasted_iota(jnp.int32, (rows, win), 0)
    q2s[1] = jnp.where(r == 0, yd, yu)
    sum2 = rcopy(q2s, q2r, SUM2, m, far_lay)
    sum2.start()

    sum1.wait()
    q1r[...] += q1s[...]
    h1_up = (q1r.at[:, last, :], h1dn, H1_UP)
    h1_dn = (q1r.at[:, first, :], h1up, H1_DN)
    to_up(*h1_up)
    to_dn(*h1_dn)
    sum2.wait()
    q2r[...] += q2s[...]
    h2_up = (q2r.at[:, last, :], h2dn, H2_UP)
    h2_dn = (q2r.at[:, first, :], h2up, H2_DN)
    to_up(*h2_up)
    to_dn(*h2_dn)

    def ext(dn, mid, up):
        return jnp.concatenate([dn, mid, up], axis=0)

    done_up(*e_up)
    done_dn(*e_dn)
    diff, obs, mask, u, v = [ext(edn[i], es[i], eup[i]) for i in range(5)]
    done_up(*h1_up)
    done_dn(*h1_dn)
    dg, cx, cy = [ext(h1dn[i], q1r[i], h1up[i]) for i in range(3)]

    def down(x):
        return pltpu.roll(x, 1, 0)

    def up(x):
        return pltpu.roll(x, x.shape[0] - 1, 0)

    wl = jnp.maximum(u, 0.0) * cx
    wr = jnp.maximum(-u, 0.0) * lane(cx, -1)
    wd = jnp.maximum(v, 0.0) * cy
    wu = jnp.maximum(-v, 0.0) * up(cy)

    def apply(f):
        return dg * f + wl * lane(f, 1) + wr * lane(f, -1) + wd * down(f) + wu * up(f)

    def adjoint(f):
        return dg * f + lane(wl * f, -1) + lane(wr * f, 1) + up(wd * f) + down(wu * f)

    done_up(*h2_up)
    done_dn(*h2_dn)
    b0 = ext(h2dn[0], q2r[0], h2up[0])
    rr = lax.broadcasted_iota(jnp.int32, b0.shape, 0)
    edge = ext(h2dn[1], q2r[1], h2up[1])
    from_dn = jnp.maximum(v, 0.0) * down(edge)
    from_up = jnp.maximum(-v, 0.0) * up(edge)
    b0 = b0 + jnp.where((rr == HALO) | (rr == HALO + rows), from_dn, 0.0)
    b0 = b0 + jnp.where((rr == HALO - 1) | (rr == HALO + rows - 1), from_up, 0.0)

    grad = beta * adjoint(mask * (b0 - obs)) + RHO * diff
    direc = -grad
    dbase = beta * apply(direc)
    hess = beta * adjoint(mask * dbase) + RHO * direc
    dhess = beta * apply(hess)

    def own(x):
        return x[HALO:HALO + rows]

    g_o, h_o, b_o, e_o, m_o = own(grad), own(hess), own(dbase), own(dhess), own(mask)
    fields[0] = fx
    fields[1] = own(b0)
    fields[2] = g_o
    fields[3] = h_o
    fields[4] = b_o
    fields[5] = e_o
    sends_tile = y == c
    send_at = pl.multiple_of(jnp.where(c == 0, part, 2 * part - step_win), 128)
    keep_at = pl.multiple_of(jnp.where(c == 0, 0, 3 * part - step_win), 128)
    tile_copy = rcopy(fields.at[:, :, pl.ds(send_at, part)], tile, TILE, m, core_lay)

    col = lax.broadcasted_iota(jnp.int32, (rows, win), 1) + mine
    inside = (col >= c * (width // 2)) & (col < (c + 1) * (width // 2))
    li = lax.broadcasted_iota(jnp.int32, (1, 128), 1)
    line = jnp.zeros((1, 128), F32)
    terms = (g_o * g_o, m_o * b_o * b_o, g_o * h_o, h_o * h_o, m_o * b_o * e_o, m_o * e_o * e_o)
    for i, x in enumerate(terms):
        s = jnp.sum(jnp.where(inside, x, 0.0), axis=(0, 1), keepdims=True)
        line = line + jnp.where(li == i, s, 0.0)
    sc_s[...] = line

    def sc_copy(d):
        mm, ll = peer(d)
        return pltpu.make_async_remote_copy(
            src_ref=sc_s, dst_ref=sc_r.at[d], send_sem=sc_ssem.at[d], recv_sem=sc_rsem.at[d],
            device_id={"map": mm, "lay": ll}, device_id_type=MESH)

    def sc_start(d, carry):
        sc_copy(d).start()
        return carry

    lax.fori_loop(1, ngroup, sc_start, 0)

    @pl.when(sends_tile)
    def _():
        tile_copy.start()
        tile[...] = fields[:, :, pl.ds(keep_at, part)]
        tile_copy.wait_send()

    @pl.when(jnp.logical_not(sends_tile))
    def _():
        tile_copy.wait_recv()

    def sc_wait(d, total):
        sc_copy(d).wait()
        return total + sc_r[d]

    total = lax.fori_loop(1, ngroup, sc_wait, line)

    def pick(i):
        return jnp.sum(jnp.where(li == i, total, 0.0), axis=1, keepdims=True)

    gg0, cv0, gh, hh, ce, ee = [pick(i) for i in range(6)]
    alpha0 = gg0 / (cv0 + RHO * gg0)
    gg1 = jnp.maximum(gg0 + alpha0 * (2.0 * gh + alpha0 * hh), 0.0)
    cv1 = jnp.maximum(cv0 - alpha0 * (2.0 * ce - alpha0 * ee), 0.0)
    den1 = cv1 + RHO * gg1
    alpha1 = jnp.where(den1 > 0.0, gg1 / jnp.where(den1 > 0.0, den1, 1.0), 0.0)
    flux1 = tile[0] - alpha0 * tile[2]
    flux_out[...] = flux1 - alpha1 * (tile[2] + alpha0 * tile[3])
    basal1 = tile[1] + alpha0 * tile[4]
    basal_out[...] = basal1 + alpha1 * (tile[4] - alpha0 * tile[5])


def shards(
    temp_start, heating, phase, velocity, surface, flux_start, flux_prior, basal_obs, obs_mask
):
    nzd, rows, width = temp_start.shape
    nmap = lax.axis_size("map")
    nlay = lax.axis_size("lay")
    win = width // 2 + MARGIN
    half = 2 * nzd
    part = width // nlay

    def buf(*shape):
        return pltpu.VMEM(shape, F32)

    scratch = [
        pltpu.VMEM((half, rows, win), jnp.int32),
        buf(nzd, rows, width),
        buf(half, rows, win),
        buf(nzd, rows, width),
        buf(half, rows, win),
        buf(nzd, 1, width), buf(nzd, 1, width),
    ] + [buf(half, rows, win)] * 9 + [
        buf(half, 1, win), buf(half, 1, win),
        buf(3, rows, win), buf(3, rows, win),
        buf(rows, win), buf(rows, win),
        buf(3, rows, win), buf(3, rows, win),
        buf(2, rows, win), buf(2, rows, win),
        buf(3, HALO, win), buf(3, HALO, win),
        buf(2, HALO, win), buf(2, HALO, win),
        buf(3, rows, width),
        pltpu.VMEM((rows, width), jnp.int32),
        buf(5, rows, win),
        buf(5, HALO, win), buf(5, HALO, win),
        buf(6, rows, win),
        buf(6, rows, part),
        buf(1, 128),
        buf(2 * nmap, 1, 128),
        pltpu.SemaphoreType.DMA((NSEM,)),
        pltpu.SemaphoreType.DMA((NSEM,)),
        pltpu.SemaphoreType.DMA((7,)),
        pltpu.SemaphoreType.DMA((2 * nmap,)),
        pltpu.SemaphoreType.DMA((2 * nmap,)),
    ]
    vmem = pl.BlockSpec(memory_space=pltpu.VMEM)
    out = jax.ShapeDtypeStruct((rows, part), F32)
    return pl.pallas_call(
        functools.partial(kernel, nmap, nlay),
        out_shape=(out, out),
        in_specs=[vmem] * 9,
        out_specs=(vmem, vmem),
        scratch_shapes=scratch,
        compiler_params=pltpu.CompilerParams(collective_id=0, has_side_effects=True),
    )(temp_start, heating, phase, velocity, surface, flux_start, flux_prior, basal_obs, obs_mask)


def solution(mesh):
    return jax.shard_map(
        shards,
        mesh=mesh,
        in_specs=(
            P("lay", "map", None),
            P("lay", "map", None),
            P("lay", "map", None),
            P(None, "map", None),
            P("map", None),
            P("map", "lay"),
            P("map", "lay"),
            P("map", "lay"),
            P("map", "lay"),
        ),
        out_specs=(P("map", "lay"), P("map", "lay")),
        check_vma=False,
    )
```

```python
import functools

import jax
import jax.numpy as jnp
from jax import lax
from jax.experimental import pallas as pl
from jax.experimental.pallas import tpu as pltpu
from jax.sharding import PartitionSpec as P

MESH = pl.DeviceIdType.MESH
F32 = jnp.float32
MARGIN = 128
HALO = 4
RHO = 0.5
(PHASE, HEAT, RHS, T_DN, T_UP, G_DN, G_UP, MEET1, MEET2, SUM1, SUM2,
 E_DN, E_UP, H1_DN, H1_UP, H2_DN, H2_UP, TILE, MAPS) = range(19)
NSEM = MAPS + 12


def lane(x, shift):
    n = x.shape[-1]
    col = lax.broadcasted_iota(jnp.int32, x.shape, x.ndim - 1)
    edge = 0 if shift > 0 else n - 1
    return jnp.where(col == edge, 0.0, pltpu.roll(x, shift % n, x.ndim - 1))


def row(x, shift, fill):
    n = x.shape[0]
    r = lax.broadcasted_iota(jnp.int32, x.shape, 0)
    edge = 0 if shift > 0 else n - 1
    return jnp.where(r == edge, fill, pltpu.roll(x, shift % n, 0))


def kernel(
    nmap, nlay,
    temp_h, heating_h, phase, velocity_h, surface_h, flux_in, prior_in, obs_in, mask_in,
    out,
    temp, heating, velocity, surface, top,
    pb, hf, hb, rf, rb, tdn, tup, inv, cc, yy, gg, sgl, sgr, sgu, sgd, wg, gdn, gup,
    m1s, m1r, m2s, m2r, q1s, q1r, q2s, q2r, h1dn, h1up, h2dn, h2up,
    maps, maski, es, edn, eup, fields, tile, sc_s, sc_r,
    ssem, rsem, lsem, sc_ssem, sc_rsem,
):
    nzd, rows, width = temp_h.shape
    win = pb.shape[2]
    depth = nzd * nlay
    half = 2 * nzd
    part = flux_in.shape[1]
    rcoef = depth * depth / 4.0
    dtime = rcoef / (depth * depth)
    beta = rcoef / depth
    m = lax.axis_index("map")
    lay = lax.axis_index("lay")
    y = lay // 2
    c = lay % 2
    core_lay = y * 2 + (1 - c)
    far_lay = (1 - y) * 2 + c
    step_win = width - win
    mine = pl.multiple_of(c * step_win, 128)
    theirs = pl.multiple_of((1 - c) * step_win, 128)
    has_dn = m > 0
    has_up = m < nmap - 1

    def slot(j):
        return jnp.where(y == 0, j, half - 1 - j)

    def rcopy(src, dst, k, mm, ll):
        return pltpu.make_async_remote_copy(
            src_ref=src, dst_ref=dst, send_sem=ssem.at[k], recv_sem=rsem.at[k],
            device_id={"map": mm, "lay": ll}, device_id_type=MESH)

    loads = [
        pltpu.make_async_copy(src, dst, lsem.at[7 + i])
        for i, (src, dst) in enumerate((
            (heating_h, heating), (phase.at[nzd - 1], top), (surface_h, surface),
            (temp_h, temp), (velocity_h, velocity)))
    ]
    ph_own = pltpu.make_async_copy(
        phase.at[:, :, pl.ds(mine, win)], pb.at[pl.ds(c * nzd, nzd)], lsem.at[0])
    ph_own.start()
    for load in loads:
        load.start()

    ngroup = 2 * nmap
    me_g = m * 2 + c

    def peer(d):
        g = lax.rem(me_g + d, ngroup)
        return g // 2, y * 2 + lax.rem(g, 2)

    barrier = pltpu.get_barrier_semaphore()

    def greet(d, carry):
        mm, ll = peer(d)
        pl.semaphore_signal(barrier, inc=1, device_id={"map": mm, "lay": ll}, device_id_type=MESH)
        return carry

    lax.fori_loop(1, ngroup, greet, 0)
    for ll in (far_lay, (1 - y) * 2 + (1 - c)):
        pl.semaphore_signal(barrier, inc=1, device_id={"map": m, "lay": ll}, device_id_type=MESH)
    pl.semaphore_wait(barrier, ngroup - 1 + 2)

    both = []
    ph = rcopy(phase.at[:, :, pl.ds(theirs, win)], pb.at[pl.ds(c * nzd, nzd)], PHASE, m, core_lay)
    ph.start()

    def to_up(src, dst, k):
        @pl.when(has_up)
        def _():
            rcopy(src, dst, k, m + 1, lay).start()

    def to_dn(src, dst, k):
        @pl.when(has_dn)
        def _():
            rcopy(src, dst, k, m - 1, lay).start()

    def done_up(src, dst, k):
        @pl.when(has_up)
        def _():
            rcopy(src, dst, k, m + 1, lay).wait_send()

        @pl.when(has_dn)
        def _():
            rcopy(src, dst, k, m - 1, lay).wait_recv()

    def done_dn(src, dst, k):
        @pl.when(has_dn)
        def _():
            rcopy(src, dst, k, m - 1, lay).wait_send()

        @pl.when(has_up)
        def _():
            rcopy(src, dst, k, m + 1, lay).wait_recv()

    t_up = (temp_h.at[:, rows - 1:rows, :], tdn, T_UP)
    t_dn = (temp_h.at[:, 0:1, :], tup, T_DN)
    to_up(*t_up)
    to_dn(*t_dn)

    map_srcs = (flux_in, prior_in, obs_in, mask_in)
    here = pl.multiple_of(lay * part, 128)
    map_copies = []
    for i, src in enumerate(map_srcs):
        dst = maski.at[:, pl.ds(here, part)] if i == 3 else maps.at[i, :, pl.ds(here, part)]
        own = pltpu.make_async_copy(src, dst, lsem.at[1 + i])
        own.start()
        map_copies.append(own)
        for d in range(1, nlay):
            cp = rcopy(src, dst, MAPS + 3 * i + d - 1, m, lax.rem(lay + d, nlay))
            cp.start()
            map_copies.append(cp)

    @pl.when(jnp.logical_not(has_dn))
    def _():
        for ref in (tdn, gdn, edn, h1dn, h2dn):
            ref[...] = jnp.zeros(ref.shape, F32)

    @pl.when(jnp.logical_not(has_up))
    def _():
        for ref in (tup, gup, eup, h1up, h2up):
            ref[...] = jnp.zeros(ref.shape, F32)

    def kappa(p):
        return jnp.where(p == 1, 0.3, 1.0).astype(F32)

    for load in loads[:3]:
        load.wait()

    def heat(l, carry):
        hf[l] = dtime * heating[l].astype(F32)
        return carry

    lax.fori_loop(0, nzd, heat, 0)
    is_top = lay == nlay - 1
    hf[nzd - 1] += jnp.where(is_top, rcoef, 0.0) * kappa(top[...]) * surface[...]
    ht = rcopy(hf.at[:, :, pl.ds(theirs, win)], hb.at[pl.ds(c * nzd, nzd)], HEAT, m, core_lay)
    ht.start()
    ht_own = pltpu.make_async_copy(
        hf.at[:, :, pl.ds(mine, win)], hb.at[pl.ds(c * nzd, nzd)], lsem.at[5])
    ht_own.start()

    ph_own.wait()
    ph.wait()
    kap0 = kappa(pb[slot(0)])
    q0 = jnp.where(y == 1, rcoef, 0.0) * kap0
    g0 = jnp.where(y == 0, 1.0, 0.0) * jnp.ones_like(kap0)

    def eliminate(j, carry):
        kap, q, yg = carry
        kap_next = kappa(pb[slot(j + 1)])
        n = (0.5 * rcoef) * (kap + kap_next)
        iv = 1.0 / (1.0 + q + n)
        cj = n * iv
        inv[j] = iv
        cc[j] = cj
        yy[j] = yg
        return kap_next, cj * (1.0 + q), cj * yg

    kap_m, q_m, yg_m = lax.fori_loop(0, half - 1, eliminate, (kap0, q0, g0))
    m1s[0] = kap_m
    m1s[1] = 1.0 + q_m
    m1s[2] = yg_m
    meet1 = rcopy(m1s, m1r, MEET1, m, far_lay)
    meet1.start()

    for load in loads[3:]:
        load.wait()
    done_up(*t_up)
    done_dn(*t_dn)

    def advect(l, carry):
        t = temp[l]
        z = (lay * nzd + l).astype(F32)
        sh = 0.3 + 0.7 * (z + 0.5) / depth
        u = velocity[0]
        v = velocity[1]
        flow = (
            jnp.maximum(u, 0.0) * lane(t, 1)
            + jnp.maximum(-u, 0.0) * lane(t, -1)
            + jnp.maximum(v, 0.0) * row(t, 1, tdn[l])
            + jnp.maximum(-v, 0.0) * row(t, -1, tup[l])
            - (jnp.abs(u) + jnp.abs(v)) * t
        )
        rf[l] = t + sh * flow + hf[l]
        return carry

    lax.fori_loop(0, nzd, advect, 0)
    rh = rcopy(rf.at[:, :, pl.ds(theirs, win)], rb.at[pl.ds(c * nzd, nzd)], RHS, m, core_lay)
    rh.start()
    rh_own = pltpu.make_async_copy(
        rf.at[:, :, pl.ds(mine, win)], rb.at[pl.ds(c * nzd, nzd)], lsem.at[6])
    rh_own.start()

    meet1.wait()
    n_mid = (0.5 * rcoef) * (kap_m + m1r[0])
    d_own = m1s[1] + n_mid
    d_far = m1r[1] + n_mid
    idet = 1.0 / (d_own * d_far - n_mid * n_mid)
    w_own = d_far * idet
    w_far = n_mid * idet
    gm = w_own * m1s[2] + w_far * m1r[2]
    gg[slot(half - 1)] = gm

    def back_g(i, x):
        j = half - 2 - i
        x = yy[j] * inv[j] + cc[j] * x
        gg[slot(j)] = x
        return x

    lax.fori_loop(0, half - 1, back_g, gm)
    g_up = (gg.at[:, rows - 1:rows, :], gdn, G_UP)
    g_dn = (gg.at[:, 0:1, :], gup, G_DN)
    to_up(*g_up)
    to_dn(*g_dn)

    for cp in map_copies:
        cp.wait()
    fx = maps[0, :, pl.ds(mine, win)]
    ob = maps[2, :, pl.ds(mine, win)]
    uw = velocity[0, :, pl.ds(mine, win)]
    vw = velocity[1, :, pl.ds(mine, win)]
    es[0] = fx - maps[1, :, pl.ds(mine, win)]
    es[1] = ob
    es[2] = maski[:, pl.ds(mine, win)].astype(F32)
    es[3] = uw
    es[4] = vw
    last = slice(rows - HALO, rows)
    first = slice(0, HALO)
    e_up = (es.at[:, last, :], edn, E_UP)
    e_dn = (es.at[:, first, :], eup, E_DN)
    to_up(*e_up)
    to_dn(*e_dn)

    rh_own.wait()
    rh.wait()
    y0 = rb[slot(0)] + jnp.where(y == 0, beta, 0.0) * fx

    def forward(j, x):
        yy[j] = x
        return rb[slot(j + 1)] + cc[j] * x

    y_m = lax.fori_loop(0, half - 1, forward, y0)
    m2s[...] = y_m
    meet2 = rcopy(m2s, m2r, MEET2, m, far_lay)
    meet2.start()

    ht_own.wait()
    ht.wait()
    done_up(*g_up)
    done_dn(*g_dn)
    suv = jnp.abs(uw) + jnp.abs(vw)

    def profile(k, carry):
        ad, ax, ay, af = carry
        g = gg[k]
        sh = 0.3 + 0.7 * ((y * half + k).astype(F32) + 0.5) / depth
        sg = sh * g
        left = lane(sg, 1)
        below = row(sg, 1, sh * gdn[k])
        w = g - suv * sg
        sgl[k] = left
        sgr[k] = lane(sg, -1)
        sgd[k] = below
        sgu[k] = row(sg, -1, sh * gup[k])
        wg[k] = w
        return ad + w * g, ax + left * g, ay + below * g, af + g * hb[k]

    zero = jnp.zeros((rows, win), F32)
    ad, ax, ay, af = lax.fori_loop(0, half, profile, (zero, zero, zero, zero))
    base = jnp.where(y == 0, 1.0, 0.0) * gg[0]
    q1s[0] = ad + base
    q1s[1] = ax
    q1s[2] = ay
    sum1 = rcopy(q1s, q1r, SUM1, m, far_lay)
    sum1.start()

    meet2.wait()
    x_m = w_own * y_m + w_far * m2r[...]

    def products(x, k, acc):
        a0, xr, xl, yu, yd = acc
        return (a0 + wg[k] * x, xr + sgr[k] * x, xl + sgl[k] * x,
                yu + sgu[k] * x, yd + sgd[k] * x)

    def back_t(i, carry):
        x, acc = carry
        j = half - 2 - i
        x = yy[j] * inv[j] + cc[j] * x
        return x, products(x, slot(j), acc)

    acc = products(x_m, slot(half - 1), (af, zero, zero, zero, zero))
    _, (a0, xr, xl, yu, yd) = lax.fori_loop(0, half - 1, back_t, (x_m, acc))
    none = jnp.zeros((1, win), F32)
    q2s[0] = (
        a0 + beta * fx * base
        + jnp.maximum(uw, 0.0) * lane(xr, 1) + jnp.maximum(-uw, 0.0) * lane(xl, -1)
        + jnp.maximum(vw, 0.0) * row(yu, 1, none) + jnp.maximum(-vw, 0.0) * row(yd, -1, none)
    )
    r = lax.broadcasted_iota(jnp.int32, (rows, win), 0)
    q2s[1] = jnp.where(r == 0, yd, yu)
    sum2 = rcopy(q2s, q2r, SUM2, m, far_lay)
    sum2.start()

    sum1.wait()
    q1r[...] += q1s[...]
    h1_up = (q1r.at[:, last, :], h1dn, H1_UP)
    h1_dn = (q1r.at[:, first, :], h1up, H1_DN)
    to_up(*h1_up)
    to_dn(*h1_dn)
    sum2.wait()
    q2r[...] += q2s[...]
    h2_up = (q2r.at[:, last, :], h2dn, H2_UP)
    h2_dn = (q2r.at[:, first, :], h2up, H2_DN)
    to_up(*h2_up)
    to_dn(*h2_dn)

    def ext(dn, mid, up):
        return jnp.concatenate([dn, mid, up], axis=0)

    done_up(*e_up)
    done_dn(*e_dn)
    diff, obs, mask, u, v = [ext(edn[i], es[i], eup[i]) for i in range(5)]
    done_up(*h1_up)
    done_dn(*h1_dn)
    dg, cx, cy = [ext(h1dn[i], q1r[i], h1up[i]) for i in range(3)]

    def down(x):
        return pltpu.roll(x, 1, 0)

    def up(x):
        return pltpu.roll(x, x.shape[0] - 1, 0)

    wl = jnp.maximum(u, 0.0) * cx
    wr = jnp.maximum(-u, 0.0) * lane(cx, -1)
    wd = jnp.maximum(v, 0.0) * cy
    wu = jnp.maximum(-v, 0.0) * up(cy)

    def apply(f):
        return dg * f + wl * lane(f, 1) + wr * lane(f, -1) + wd * down(f) + wu * up(f)

    def adjoint(f):
        return dg * f + lane(wl * f, -1) + lane(wr * f, 1) + up(wd * f) + down(wu * f)

    done_up(*h2_up)
    done_dn(*h2_dn)
    b0 = ext(h2dn[0], q2r[0], h2up[0])
    rr = lax.broadcasted_iota(jnp.int32, b0.shape, 0)
    edge = ext(h2dn[1], q2r[1], h2up[1])
    from_dn = jnp.maximum(v, 0.0) * down(edge)
    from_up = jnp.maximum(-v, 0.0) * up(edge)
    b0 = b0 + jnp.where((rr == HALO) | (rr == HALO + rows), from_dn, 0.0)
    b0 = b0 + jnp.where((rr == HALO - 1) | (rr == HALO + rows - 1), from_up, 0.0)

    grad = beta * adjoint(mask * (b0 - obs)) + RHO * diff
    direc = -grad
    dbase = beta * apply(direc)
    hess = beta * adjoint(mask * dbase) + RHO * direc
    dhess = beta * apply(hess)

    def own(x):
        return x[HALO:HALO + rows]

    g_o, h_o, b_o, e_o, m_o = own(grad), own(hess), own(dbase), own(dhess), own(mask)
    fields[0] = fx
    fields[1] = own(b0)
    fields[2] = g_o
    fields[3] = h_o
    fields[4] = b_o
    fields[5] = e_o
    sends_tile = y == c
    send_at = pl.multiple_of(jnp.where(c == 0, part, 2 * part - step_win), 128)
    keep_at = pl.multiple_of(jnp.where(c == 0, 0, 3 * part - step_win), 128)
    tile_copy = rcopy(fields.at[:, :, pl.ds(send_at, part)], tile, TILE, m, core_lay)

    col = lax.broadcasted_iota(jnp.int32, (rows, win), 1) + mine
    inside = (col >= c * (width // 2)) & (col < (c + 1) * (width // 2))
    li = lax.broadcasted_iota(jnp.int32, (1, 128), 1)
    line = jnp.zeros((1, 128), F32)
    terms = (g_o * g_o, m_o * b_o * b_o, g_o * h_o, h_o * h_o, m_o * b_o * e_o, m_o * e_o * e_o)
    for i, x in enumerate(terms):
        s = jnp.sum(jnp.where(inside, x, 0.0), axis=(0, 1), keepdims=True)
        line = line + jnp.where(li == i, s, 0.0)
    sc_s[...] = line

    def sc_copy(d):
        mm, ll = peer(d)
        return pltpu.make_async_remote_copy(
            src_ref=sc_s, dst_ref=sc_r.at[d], send_sem=sc_ssem.at[d], recv_sem=sc_rsem.at[d],
            device_id={"map": mm, "lay": ll}, device_id_type=MESH)

    def sc_start(d, carry):
        sc_copy(d).start()
        return carry

    lax.fori_loop(1, ngroup, sc_start, 0)

    @pl.when(sends_tile)
    def _():
        tile_copy.start()
        tile[...] = fields[:, :, pl.ds(keep_at, part)]
        tile_copy.wait_send()

    @pl.when(jnp.logical_not(sends_tile))
    def _():
        tile_copy.wait_recv()

    def sc_wait(d, total):
        sc_copy(d).wait()
        return total + sc_r[d]

    total = lax.fori_loop(1, ngroup, sc_wait, line)

    def pick(i):
        return jnp.sum(jnp.where(li == i, total, 0.0), axis=1, keepdims=True)

    gg0, cv0, gh, hh, ce, ee = [pick(i) for i in range(6)]
    alpha0 = gg0 / (cv0 + RHO * gg0)
    gg1 = jnp.maximum(gg0 + alpha0 * (2.0 * gh + alpha0 * hh), 0.0)
    cv1 = jnp.maximum(cv0 - alpha0 * (2.0 * ce - alpha0 * ee), 0.0)
    den1 = cv1 + RHO * gg1
    alpha1 = jnp.where(den1 > 0.0, gg1 / jnp.where(den1 > 0.0, den1, 1.0), 0.0)
    flux1 = tile[0] - alpha0 * tile[2]
    out[0] = flux1 - alpha1 * (tile[2] + alpha0 * tile[3])
    basal1 = tile[1] + alpha0 * tile[4]
    out[1] = basal1 + alpha1 * (tile[4] - alpha0 * tile[5])


def shards(
    temp_start, heating, phase, velocity, surface, flux_start, flux_prior, basal_obs, obs_mask
):
    nzd, rows, width = temp_start.shape
    nmap = lax.axis_size("map")
    nlay = lax.axis_size("lay")
    win = width // 2 + MARGIN
    half = 2 * nzd
    part = width // nlay

    def buf(*shape):
        return pltpu.VMEM(shape, F32)

    scratch = [
        buf(nzd, rows, width), pltpu.VMEM((nzd, rows, width), heating.dtype),
        buf(2, rows, width), buf(rows, width),
        pltpu.VMEM((rows, width), jnp.int32),
        pltpu.VMEM((half, rows, win), jnp.int32),
        buf(nzd, rows, width),
        buf(half, rows, win),
        buf(nzd, rows, width),
        buf(half, rows, win),
        buf(nzd, 1, width), buf(nzd, 1, width),
    ] + [buf(half, rows, win)] * 9 + [
        buf(half, 1, win), buf(half, 1, win),
        buf(3, rows, win), buf(3, rows, win),
        buf(rows, win), buf(rows, win),
        buf(3, rows, win), buf(3, rows, win),
        buf(2, rows, win), buf(2, rows, win),
        buf(3, HALO, win), buf(3, HALO, win),
        buf(2, HALO, win), buf(2, HALO, win),
        buf(3, rows, width),
        pltpu.VMEM((rows, width), jnp.int32),
        buf(5, rows, win),
        buf(5, HALO, win), buf(5, HALO, win),
        buf(6, rows, win),
        buf(6, rows, part),
        buf(1, 128),
        buf(2 * nmap, 1, 128),
        pltpu.SemaphoreType.DMA((NSEM,)),
        pltpu.SemaphoreType.DMA((NSEM,)),
        pltpu.SemaphoreType.DMA((12,)),
        pltpu.SemaphoreType.DMA((2 * nmap,)),
        pltpu.SemaphoreType.DMA((2 * nmap,)),
    ]
    vmem = pl.BlockSpec(memory_space=pltpu.VMEM)
    any_ = pl.BlockSpec(memory_space=pl.ANY)
    out = pl.pallas_call(
        functools.partial(kernel, nmap, nlay),
        out_shape=jax.ShapeDtypeStruct((2, rows, part), F32),
        in_specs=[any_] * 9,
        out_specs=vmem,
        scratch_shapes=scratch,
        compiler_params=pltpu.CompilerParams(collective_id=0, has_side_effects=True),
    )(temp_start, heating, phase, velocity, surface, flux_start, flux_prior, basal_obs, obs_mask)
    return out[0], out[1]


def solution(mesh):
    return jax.shard_map(
        shards,
        mesh=mesh,
        in_specs=(
            P("lay", "map", None),
            P("lay", "map", None),
            P("lay", "map", None),
            P(None, "map", None),
            P("map", None),
            P("map", "lay"),
            P("map", "lay"),
            P("map", "lay"),
            P("map", "lay"),
        ),
        out_specs=(P("map", "lay"), P("map", "lay")),
        check_vma=False,
    )
```

```python
import functools

import jax
import jax.numpy as jnp
from jax import lax
from jax.experimental import pallas as pl
from jax.experimental.pallas import tpu as pltpu
from jax.sharding import PartitionSpec as P

MESH = pl.DeviceIdType.MESH
F32 = jnp.float32
MARGIN = 128
HALO = 4
RHO = 0.5
(PHASE, HEAT, RHS, T_DN, T_UP, G_DN, G_UP, MEET1, MEET2, SUM1, SUM2,
 E_DN, E_UP, H1_DN, H1_UP, H2_DN, H2_UP, TILE, SUM3, H3_DN, H3_UP, MAPS) = range(22)
NSEM = MAPS + 12


def lane(x, shift):
    n = x.shape[-1]
    col = lax.broadcasted_iota(jnp.int32, x.shape, x.ndim - 1)
    edge = 0 if shift > 0 else n - 1
    return jnp.where(col == edge, 0.0, pltpu.roll(x, shift % n, x.ndim - 1))


def row(x, shift, fill):
    n = x.shape[0]
    r = lax.broadcasted_iota(jnp.int32, x.shape, 0)
    edge = 0 if shift > 0 else n - 1
    return jnp.where(r == edge, fill, pltpu.roll(x, shift % n, 0))


def kernel(
    nmap, nlay,
    temp_h, heating_h, phase, velocity_h, surface_h, flux_in, prior_in, obs_in, mask_in,
    out,
    temp, heating, velocity, surface, top,
    pb, hf, hb, rf, rb, tdn, tup, inv, cc, yy, gg, sgl, sgr, wg, gdn, gup,
    m1s, m1r, m2s, m2r, q1s, q1r, q2s, q2r, h1dn, h1up, h2dn, h2up, q3s, q3r, h3dn, h3up,
    maps, maski, es, edn, eup, fields, tile, sc_s, sc_r,
    ssem, rsem, lsem, sc_ssem, sc_rsem,
):
    nzd, rows, width = temp_h.shape
    win = pb.shape[2]
    depth = nzd * nlay
    half = 2 * nzd
    part = flux_in.shape[1]
    rcoef = depth * depth / 4.0
    dtime = rcoef / (depth * depth)
    beta = rcoef / depth
    m = lax.axis_index("map")
    lay = lax.axis_index("lay")
    y = lay // 2
    c = lay % 2
    core_lay = y * 2 + (1 - c)
    far_lay = (1 - y) * 2 + c
    step_win = width - win
    mine = pl.multiple_of(c * step_win, 128)
    theirs = pl.multiple_of((1 - c) * step_win, 128)
    has_dn = m > 0
    has_up = m < nmap - 1

    def slot(j):
        return jnp.where(y == 0, j, half - 1 - j)

    def rcopy(src, dst, k, mm, ll):
        return pltpu.make_async_remote_copy(
            src_ref=src, dst_ref=dst, send_sem=ssem.at[k], recv_sem=rsem.at[k],
            device_id={"map": mm, "lay": ll}, device_id_type=MESH)

    loads = [
        pltpu.make_async_copy(src, dst, lsem.at[7 + i])
        for i, (src, dst) in enumerate((
            (heating_h, heating), (phase.at[nzd - 1], top), (surface_h, surface),
            (temp_h, temp), (velocity_h, velocity)))
    ]
    ph_own = pltpu.make_async_copy(
        phase.at[:, :, pl.ds(mine, win)], pb.at[pl.ds(c * nzd, nzd)], lsem.at[0])
    ph_own.start()
    for load in loads:
        load.start()

    ngroup = 2 * nmap
    me_g = m * 2 + c

    def peer(d):
        g = lax.rem(me_g + d, ngroup)
        return g // 2, y * 2 + lax.rem(g, 2)

    barrier = pltpu.get_barrier_semaphore()

    def greet(d, carry):
        mm, ll = peer(d)
        pl.semaphore_signal(barrier, inc=1, device_id={"map": mm, "lay": ll}, device_id_type=MESH)
        return carry

    lax.fori_loop(1, ngroup, greet, 0)
    for ll in (far_lay, (1 - y) * 2 + (1 - c)):
        pl.semaphore_signal(barrier, inc=1, device_id={"map": m, "lay": ll}, device_id_type=MESH)
    pl.semaphore_wait(barrier, ngroup - 1 + 2)

    ph = rcopy(phase.at[:, :, pl.ds(theirs, win)], pb.at[pl.ds(c * nzd, nzd)], PHASE, m, core_lay)
    ph.start()

    def to_up(src, dst, k):
        @pl.when(has_up)
        def _():
            rcopy(src, dst, k, m + 1, lay).start()

    def to_dn(src, dst, k):
        @pl.when(has_dn)
        def _():
            rcopy(src, dst, k, m - 1, lay).start()

    def done_up(src, dst, k):
        @pl.when(has_up)
        def _():
            rcopy(src, dst, k, m + 1, lay).wait_send()

        @pl.when(has_dn)
        def _():
            rcopy(src, dst, k, m - 1, lay).wait_recv()

    def done_dn(src, dst, k):
        @pl.when(has_dn)
        def _():
            rcopy(src, dst, k, m - 1, lay).wait_send()

        @pl.when(has_up)
        def _():
            rcopy(src, dst, k, m + 1, lay).wait_recv()

    t_up = (temp_h.at[:, rows - 1:rows, :], tdn, T_UP)
    t_dn = (temp_h.at[:, 0:1, :], tup, T_DN)
    to_up(*t_up)
    to_dn(*t_dn)

    map_srcs = (flux_in, prior_in, obs_in, mask_in)
    here = pl.multiple_of(lay * part, 128)
    map_copies = []
    for i, src in enumerate(map_srcs):
        dst = maski.at[:, pl.ds(here, part)] if i == 3 else maps.at[i, :, pl.ds(here, part)]
        own = pltpu.make_async_copy(src, dst, lsem.at[1 + i])
        own.start()
        map_copies.append(own)
        for d in range(1, nlay):
            cp = rcopy(src, dst, MAPS + 3 * i + d - 1, m, lax.rem(lay + d, nlay))
            cp.start()
            map_copies.append(cp)

    @pl.when(jnp.logical_not(has_dn))
    def _():
        for ref in (tdn, gdn, edn, h1dn, h2dn, h3dn):
            ref[...] = jnp.zeros(ref.shape, F32)

    @pl.when(jnp.logical_not(has_up))
    def _():
        for ref in (tup, gup, eup, h1up, h2up, h3up):
            ref[...] = jnp.zeros(ref.shape, F32)

    def kappa(p):
        return jnp.where(p == 1, 0.3, 1.0).astype(F32)

    ph_own.wait()
    ph.wait()
    kap0 = kappa(pb[slot(0)])
    q0 = jnp.where(y == 1, rcoef, 0.0) * kap0
    g0 = jnp.where(y == 0, 1.0, 0.0) * jnp.ones_like(kap0)

    def eliminate(j, carry):
        kap, q, yg = carry
        kap_next = kappa(pb[slot(j + 1)])
        n = (0.5 * rcoef) * (kap + kap_next)
        iv = 1.0 / (1.0 + q + n)
        cj = n * iv
        inv[j] = iv
        cc[j] = cj
        yy[j] = yg
        return kap_next, cj * (1.0 + q), cj * yg

    kap_m, q_m, yg_m = lax.fori_loop(0, half - 1, eliminate, (kap0, q0, g0))
    m1s[0] = kap_m
    m1s[1] = 1.0 + q_m
    m1s[2] = yg_m
    meet1 = rcopy(m1s, m1r, MEET1, m, far_lay)
    meet1.start()

    for load in loads[:3]:
        load.wait()

    def heat(l, carry):
        hf[l] = dtime * heating[l].astype(F32)
        return carry

    lax.fori_loop(0, nzd, heat, 0)
    is_top = lay == nlay - 1
    hf[nzd - 1] += jnp.where(is_top, rcoef, 0.0) * kappa(top[...]) * surface[...]
    ht = rcopy(hf.at[:, :, pl.ds(theirs, win)], hb.at[pl.ds(c * nzd, nzd)], HEAT, m, core_lay)
    ht.start()
    ht_own = pltpu.make_async_copy(
        hf.at[:, :, pl.ds(mine, win)], hb.at[pl.ds(c * nzd, nzd)], lsem.at[5])
    ht_own.start()


    meet1.wait()
    n_mid = (0.5 * rcoef) * (kap_m + m1r[0])
    d_own = m1s[1] + n_mid
    d_far = m1r[1] + n_mid
    idet = 1.0 / (d_own * d_far - n_mid * n_mid)
    w_own = d_far * idet
    w_far = n_mid * idet
    gm = w_own * m1s[2] + w_far * m1r[2]
    gg[slot(half - 1)] = gm

    def back_g(i, x):
        j = half - 2 - i
        x = yy[j] * inv[j] + cc[j] * x
        gg[slot(j)] = x
        return x

    lax.fori_loop(0, half - 1, back_g, gm)
    g_up = (gg.at[:, rows - 1:rows, :], gdn, G_UP)
    g_dn = (gg.at[:, 0:1, :], gup, G_DN)
    to_up(*g_up)
    to_dn(*g_dn)

    for load in loads[3:]:
        load.wait()
    done_up(*t_up)
    done_dn(*t_dn)

    def advect(l, carry):
        t = temp[l]
        z = (lay * nzd + l).astype(F32)
        sh = 0.3 + 0.7 * (z + 0.5) / depth
        u = velocity[0]
        v = velocity[1]
        flow = (
            jnp.maximum(u, 0.0) * lane(t, 1)
            + jnp.maximum(-u, 0.0) * lane(t, -1)
            + jnp.maximum(v, 0.0) * row(t, 1, tdn[l])
            + jnp.maximum(-v, 0.0) * row(t, -1, tup[l])
            - (jnp.abs(u) + jnp.abs(v)) * t
        )
        rf[l] = t + sh * flow + hf[l]
        return carry

    lax.fori_loop(0, nzd, advect, 0)
    rh = rcopy(rf.at[:, :, pl.ds(theirs, win)], rb.at[pl.ds(c * nzd, nzd)], RHS, m, core_lay)
    rh.start()
    rh_own = pltpu.make_async_copy(
        rf.at[:, :, pl.ds(mine, win)], rb.at[pl.ds(c * nzd, nzd)], lsem.at[6])
    rh_own.start()

    for cp in map_copies:
        cp.wait()
    fx = maps[0, :, pl.ds(mine, win)]
    ob = maps[2, :, pl.ds(mine, win)]
    uw = velocity[0, :, pl.ds(mine, win)]
    vw = velocity[1, :, pl.ds(mine, win)]
    es[0] = fx - maps[1, :, pl.ds(mine, win)]
    es[1] = ob
    es[2] = maski[:, pl.ds(mine, win)].astype(F32)
    es[3] = uw
    es[4] = vw
    last = slice(rows - HALO, rows)
    first = slice(0, HALO)
    e_up = (es.at[:, last, :], edn, E_UP)
    e_dn = (es.at[:, first, :], eup, E_DN)

    rh_own.wait()
    rh.wait()
    y0 = rb[slot(0)] + jnp.where(y == 0, beta, 0.0) * fx

    def forward(j, x):
        yy[j] = x
        return rb[slot(j + 1)] + cc[j] * x

    y_m = lax.fori_loop(0, half - 1, forward, y0)
    m2s[...] = y_m
    meet2 = rcopy(m2s, m2r, MEET2, m, far_lay)
    meet2.start()

    ht_own.wait()
    ht.wait()
    suv = jnp.abs(uw) + jnp.abs(vw)

    def profile(k, carry):
        ad, ax, af = carry
        g = gg[k]
        sh = 0.3 + 0.7 * ((y * half + k).astype(F32) + 0.5) / depth
        sg = sh * g
        left = lane(sg, 1)
        w = g - suv * sg
        sgl[k] = left
        sgr[k] = lane(sg, -1)
        wg[k] = w
        return ad + w * g, ax + left * g, af + g * hb[k]

    zero = jnp.zeros((rows, win), F32)
    ad, ax, af = lax.fori_loop(0, half, profile, (zero, zero, zero))
    base = jnp.where(y == 0, 1.0, 0.0) * gg[0]
    q1s[0] = ad + base
    q1s[1] = ax
    sum1 = rcopy(q1s, q1r, SUM1, m, far_lay)
    sum1.start()

    done_up(*g_up)
    done_dn(*g_dn)
    to_up(*e_up)
    to_dn(*e_dn)
    meet2.wait()
    x_m = w_own * y_m + w_far * m2r[...]

    def products(x, k, acc):
        a0, xr, xl, yu, yd, ay = acc
        g = gg[k]
        sh = 0.3 + 0.7 * ((y * half + k).astype(F32) + 0.5) / depth
        sx = sh * x
        below = row(g, 1, gdn[k])
        return (a0 + wg[k] * x, xr + sgr[k] * x, xl + sgl[k] * x,
                yu + row(g, -1, gup[k]) * sx, yd + below * sx, ay + below * (sh * g))

    def back_t(i, carry):
        x, acc = carry
        j = half - 2 - i
        x = yy[j] * inv[j] + cc[j] * x
        return x, products(x, slot(j), acc)

    acc = products(x_m, slot(half - 1), (af, zero, zero, zero, zero, zero))
    _, (a0, xr, xl, yu, yd, ay) = lax.fori_loop(0, half - 1, back_t, (x_m, acc))
    none = jnp.zeros((1, win), F32)
    q2s[0] = (
        a0 + beta * fx * base
        + jnp.maximum(uw, 0.0) * lane(xr, 1) + jnp.maximum(-uw, 0.0) * lane(xl, -1)
        + jnp.maximum(vw, 0.0) * row(yu, 1, none) + jnp.maximum(-vw, 0.0) * row(yd, -1, none)
    )
    q2s[1] = ay
    sum2 = rcopy(q2s, q2r, SUM2, m, far_lay)
    sum2.start()
    q3s[0] = yd[0:1]
    q3s[1] = yu[rows - 1:rows]
    sum3 = rcopy(q3s, q3r, SUM3, m, far_lay)
    sum3.start()

    sum1.wait()
    q1r[...] += q1s[...]
    h1_up = (q1r.at[:, last, :], h1dn, H1_UP)
    h1_dn = (q1r.at[:, first, :], h1up, H1_DN)
    to_up(*h1_up)
    to_dn(*h1_dn)
    sum2.wait()
    q2r[...] += q2s[...]
    h2_up = (q2r.at[:, last, :], h2dn, H2_UP)
    h2_dn = (q2r.at[:, first, :], h2up, H2_DN)
    to_up(*h2_up)
    to_dn(*h2_dn)
    sum3.wait()
    q3r[...] += q3s[...]
    h3_up = (q3r.at[1], h3dn, H3_UP)
    h3_dn = (q3r.at[0], h3up, H3_DN)
    to_up(*h3_up)
    to_dn(*h3_dn)

    def ext(dn, mid, up):
        return jnp.concatenate([dn, mid, up], axis=0)

    done_up(*e_up)
    done_dn(*e_dn)
    diff, obs, mask, u, v = [ext(edn[i], es[i], eup[i]) for i in range(5)]
    done_up(*h1_up)
    done_dn(*h1_dn)
    dg, cx = [ext(h1dn[i], q1r[i], h1up[i]) for i in range(2)]

    def down(x):
        return pltpu.roll(x, 1, 0)

    def up(x):
        return pltpu.roll(x, x.shape[0] - 1, 0)

    wl = jnp.maximum(u, 0.0) * cx
    wr = jnp.maximum(-u, 0.0) * lane(cx, -1)

    def apply(f):
        return dg * f + wl * lane(f, 1) + wr * lane(f, -1) + wd * down(f) + wu * up(f)

    def adjoint(f):
        return dg * f + lane(wl * f, -1) + lane(wr * f, 1) + up(wd * f) + down(wu * f)

    done_up(*h2_up)
    done_dn(*h2_dn)
    b0, cy = [ext(h2dn[i], q2r[i], h2up[i]) for i in range(2)]
    wd = jnp.maximum(v, 0.0) * cy
    wu = jnp.maximum(-v, 0.0) * up(cy)
    done_up(*h3_up)
    done_dn(*h3_dn)
    rr = lax.broadcasted_iota(jnp.int32, b0.shape, 0)
    from_dn = jnp.where(rr == HALO, h3dn[...], 0.0) + jnp.where(rr == HALO + rows, q3r[1], 0.0)
    from_up = jnp.where(rr == HALO - 1, q3r[0], 0.0) + jnp.where(rr == HALO + rows - 1, h3up[...], 0.0)
    b0 = b0 + jnp.maximum(v, 0.0) * from_dn + jnp.maximum(-v, 0.0) * from_up

    grad = beta * adjoint(mask * (b0 - obs)) + RHO * diff
    direc = -grad
    dbase = beta * apply(direc)
    hess = beta * adjoint(mask * dbase) + RHO * direc
    dhess = beta * apply(hess)

    def own(x):
        return x[HALO:HALO + rows]

    g_o, h_o, b_o, e_o, m_o = own(grad), own(hess), own(dbase), own(dhess), own(mask)
    fields[0] = fx
    fields[1] = own(b0)
    fields[2] = g_o
    fields[3] = h_o
    fields[4] = b_o
    fields[5] = e_o
    sends_tile = y == c
    send_at = pl.multiple_of(jnp.where(c == 0, part, 2 * part - step_win), 128)
    keep_at = pl.multiple_of(jnp.where(c == 0, 0, 3 * part - step_win), 128)
    tile_copy = rcopy(fields.at[:, :, pl.ds(send_at, part)], tile, TILE, m, core_lay)

    col = lax.broadcasted_iota(jnp.int32, (rows, win), 1) + mine
    inside = (col >= c * (width // 2)) & (col < (c + 1) * (width // 2))
    li = lax.broadcasted_iota(jnp.int32, (1, 128), 1)
    line = jnp.zeros((1, 128), F32)
    terms = (g_o * g_o, m_o * b_o * b_o, g_o * h_o, h_o * h_o, m_o * b_o * e_o, m_o * e_o * e_o)
    for i, x in enumerate(terms):
        s = jnp.sum(jnp.where(inside, x, 0.0), axis=(0, 1), keepdims=True)
        line = line + jnp.where(li == i, s, 0.0)
    sc_s[...] = line

    def sc_copy(d):
        mm, ll = peer(d)
        return pltpu.make_async_remote_copy(
            src_ref=sc_s, dst_ref=sc_r.at[d], send_sem=sc_ssem.at[d], recv_sem=sc_rsem.at[d],
            device_id={"map": mm, "lay": ll}, device_id_type=MESH)

    def sc_start(d, carry):
        sc_copy(d).start()
        return carry

    lax.fori_loop(1, ngroup, sc_start, 0)

    @pl.when(sends_tile)
    def _():
        tile_copy.start()
        tile[...] = fields[:, :, pl.ds(keep_at, part)]
        tile_copy.wait_send()

    @pl.when(jnp.logical_not(sends_tile))
    def _():
        tile_copy.wait_recv()

    def sc_wait(d, total):
        sc_copy(d).wait()
        return total + sc_r[d]

    total = lax.fori_loop(1, ngroup, sc_wait, line)

    def pick(i):
        return jnp.sum(jnp.where(li == i, total, 0.0), axis=1, keepdims=True)

    gg0, cv0, gh, hh, ce, ee = [pick(i) for i in range(6)]
    alpha0 = gg0 / (cv0 + RHO * gg0)
    gg1 = jnp.maximum(gg0 + alpha0 * (2.0 * gh + alpha0 * hh), 0.0)
    cv1 = jnp.maximum(cv0 - alpha0 * (2.0 * ce - alpha0 * ee), 0.0)
    den1 = cv1 + RHO * gg1
    alpha1 = jnp.where(den1 > 0.0, gg1 / jnp.where(den1 > 0.0, den1, 1.0), 0.0)
    flux1 = tile[0] - alpha0 * tile[2]
    out[0] = flux1 - alpha1 * (tile[2] + alpha0 * tile[3])
    basal1 = tile[1] + alpha0 * tile[4]
    out[1] = basal1 + alpha1 * (tile[4] - alpha0 * tile[5])


def shards(
    temp_start, heating, phase, velocity, surface, flux_start, flux_prior, basal_obs, obs_mask
):
    nzd, rows, width = temp_start.shape
    nmap = lax.axis_size("map")
    nlay = lax.axis_size("lay")
    win = width // 2 + MARGIN
    half = 2 * nzd
    part = width // nlay

    def buf(*shape):
        return pltpu.VMEM(shape, F32)

    scratch = [
        buf(nzd, rows, width), pltpu.VMEM((nzd, rows, width), heating.dtype),
        buf(2, rows, width), buf(rows, width),
        pltpu.VMEM((rows, width), jnp.int32),
        pltpu.VMEM((half, rows, win), jnp.int32),
        buf(nzd, rows, width),
        buf(half, rows, win),
        buf(nzd, rows, width),
        buf(half, rows, win),
        buf(nzd, 1, width), buf(nzd, 1, width),
    ] + [buf(half, rows, win)] * 7 + [
        buf(half, 1, win), buf(half, 1, win),
        buf(3, rows, win), buf(3, rows, win),
        buf(rows, win), buf(rows, win),
        buf(2, rows, win), buf(2, rows, win),
        buf(2, rows, win), buf(2, rows, win),
        buf(2, HALO, win), buf(2, HALO, win),
        buf(2, HALO, win), buf(2, HALO, win),
        buf(2, 1, win), buf(2, 1, win), buf(1, win), buf(1, win),
        buf(3, rows, width),
        pltpu.VMEM((rows, width), jnp.int32),
        buf(5, rows, win),
        buf(5, HALO, win), buf(5, HALO, win),
        buf(6, rows, win),
        buf(6, rows, part),
        buf(1, 128),
        buf(2 * nmap, 1, 128),
        pltpu.SemaphoreType.DMA((NSEM,)),
        pltpu.SemaphoreType.DMA((NSEM,)),
        pltpu.SemaphoreType.DMA((12,)),
        pltpu.SemaphoreType.DMA((2 * nmap,)),
        pltpu.SemaphoreType.DMA((2 * nmap,)),
    ]
    vmem = pl.BlockSpec(memory_space=pltpu.VMEM)
    any_ = pl.BlockSpec(memory_space=pl.ANY)
    out = pl.pallas_call(
        functools.partial(kernel, nmap, nlay),
        out_shape=jax.ShapeDtypeStruct((2, rows, part), F32),
        in_specs=[any_] * 9,
        out_specs=vmem,
        scratch_shapes=scratch,
        compiler_params=pltpu.CompilerParams(collective_id=0, has_side_effects=True),
    )(temp_start, heating, phase, velocity, surface, flux_start, flux_prior, basal_obs, obs_mask)
    return out[0], out[1]


def solution(mesh):
    return jax.shard_map(
        shards,
        mesh=mesh,
        in_specs=(
            P("lay", "map", None),
            P("lay", "map", None),
            P("lay", "map", None),
            P(None, "map", None),
            P("map", None),
            P("map", "lay"),
            P("map", "lay"),
            P("map", "lay"),
            P("map", "lay"),
        ),
        out_specs=(P("map", "lay"), P("map", "lay")),
        check_vma=False,
    )
```
